128 devices in a mesh: stretch: 4 (over x), ctx: 32 (over y, z, core).
Axes of the slice: x: 4, y: 4, z: 4, core: 2. Of those that a mesh axis runs over, the one named last changes fastest.
Arguments:
- post_gate: bfloat16 [16384, 8192], P(('stretch', 'ctx')), may hold values from -6 to 6
- pre_gate: bfloat16 [16384, 8192], P(('stretch', 'ctx')), may hold values from -6 to 6
- values: bfloat16 [16384, 8192], P(('stretch', 'ctx')), may hold values from -6 to 6
- filters: float32 [256, 4096], P('ctx'), may hold values from -0.09375 to 0.09375
- skip_bias: float32 [8192], P('ctx'), may hold values from -1 to 1
- doc_blocks: int32 [16], replicated, may hold values from 1 to 48, 128 in all
Outputs:
- output: bfloat16 [16384, 8192], P(('stretch', 'ctx'))
The draws below stay inside these ranges and needn't reach their ends.
Inputs may be any that keep to these rules, and one draw needn't show every extreme that they name: doc_blocks sum to 128; the largest is exactly 48.
All inputs are finite; a program needn't handle non-finite values.
Results may differ from the reference program's by a relative error of at most 0.0057.
Values may be sent and summed in bfloat16 or wider, within the bound.
No kernel may reach another device: no remote copies, remote signals or barrier semaphores. Data moves between devices by JAX's collectives and lax.ppermute only.
A program may use at most 128 MiB of HBM per device.

```python
import math
import jax
import jax.numpy as jnp
import numpy as np
from jax import lax

D = 8192
GROUPS = 256
FLEN = 4096
BLK = 128
NDOC = 16
TOKENS = 16384
MAXB = 48


def block_levels(key, shape, split, low, high):
    def one(dim, blocks):
        heights = jax.random.uniform(jax.random.fold_in(jax.random.fold_in(key, 6), dim), (blocks,), jnp.float32, low / len(split), high / len(split))
        return jnp.repeat(jnp.exp(heights), shape[dim] // blocks).reshape((-1,) + (1,) * (len(shape) - dim - 1))

    factor_of = one(*split[0])
    for cut in split[1:]:
        factor_of = factor_of * one(*cut)
    return factor_of


def profile(amount, total, bound, skew):
    weights = [(1 << 20) // math.isqrt(rank ** skew) + 1 for rank in range(2, amount + 1)]
    rest, given = total - bound - (amount - 1), [1] * (amount - 1)
    while rest > 0:
        movable = [i for i in range(amount - 1) if given[i] < bound]
        mass, left = sum([weights[i] for i in movable]), rest
        for i in movable:
            addition = min(bound - given[i], max(1, left * weights[i] // mass), rest)
            given[i] = given[i] + addition
            rest = rest - addition
    return np.array([bound] + given)


def uneven_parts(key, number_of, total, bound, slope):
    if number_of == 2:
        one = jax.random.randint(key, (), max(1, total - bound), min(bound, total - 1) + 1)
        return jnp.stack([one, total - one])
    tallies = jnp.asarray(profile(number_of, total, bound, slope), jnp.int32)
    pairs = (number_of - 1) // 2
    source_of, receiver = tallies[1:1 + 2 * pairs:2], tallies[2:2 + 2 * pairs:2]
    margin = jnp.minimum(source_of - 1, bound - receiver)
    passed = jax.random.randint(jax.random.fold_in(key, 1), (pairs,), 0, 1 << 20) % (margin + 1)
    tallies = tallies.at[1:1 + 2 * pairs:2].set(source_of - passed).at[2:2 + 2 * pairs:2].set(receiver + passed)
    return tallies[jax.random.permutation(jax.random.fold_in(key, 2), number_of)]


def noise(own_key, dims, deviation, reach, cuts=(), kind=jnp.bfloat16):
    result = jax.random.normal(own_key, dims, jnp.float32) * deviation
    if len(cuts) > 0:
        result = block_levels(own_key, dims, cuts, -0.22, 0.18) * result
    return jnp.clip(result, min=-reach, max=reach).astype(kind)


def setup_inputs(seed: int = 0) -> dict:
    seeds = jax.random.split(jax.random.key(seed), 7)
    return {
        "post_gate": noise(seeds[0], (TOKENS, D), 1.0, 6.0, ((0, 128),)),
        "pre_gate": noise(seeds[1], (TOKENS, D), 1.0, 6.0, ((0, 128),)),
        "values": noise(seeds[2], (TOKENS, D), 1.0, 6.0, ((0, 128),)),
        "filters": noise(seeds[3], (GROUPS, FLEN), FLEN ** -0.5, 0.09375, ((0, 32),), jnp.float32),
        "skip_bias": jnp.clip(jax.random.uniform(seeds[4], (D,), jnp.float32, -1.0, 1.0) * block_levels(seeds[4], (D,), ((0, 32),), -0.4, 0.0), -1.0, 1.0),
        "doc_blocks": uneven_parts(seeds[5], NDOC, TOKENS // BLK, MAXB, 2).astype(jnp.int32),
    }


def block_starts(doc_blocks, block_ids):
    doc_ends = jnp.cumsum(doc_blocks)
    before = doc_ends[None, :] <= block_ids[:, None]
    return jnp.sum(jnp.where(before, doc_blocks[None, :], 0), axis=1)


def reference(post_gate, pre_gate, values, filters, skip_bias, doc_blocks):
    tokens = post_gate.shape[0]
    all_blocks = tokens // BLK
    lag_blocks = FLEN // BLK + 1
    group_width = D // GROUPS
    gated = (pre_gate.astype(jnp.float32) * values.astype(jnp.float32)).astype(jnp.bfloat16)
    block_ids = jnp.arange(all_blocks, dtype=jnp.int32)
    starts = block_starts(doc_blocks, block_ids)
    lag_ids = jnp.arange(lag_blocks, dtype=jnp.int32)
    sources = block_ids[:, None] - lag_ids[None, :]
    live_pairs = (sources >= starts[:, None]).astype(jnp.float32)
    row_ids = jnp.arange(BLK, dtype=jnp.int32)
    tap_index = lag_ids[None, :, None] * BLK + row_ids[:, None, None] - row_ids[None, None, :]
    inside = (tap_index >= 0) & (tap_index < FLEN)
    clipped = jnp.clip(tap_index, 0, FLEN - 1)
    padded = jnp.concatenate([jnp.zeros((FLEN, D), gated.dtype), gated], axis=0)
    grouped = padded.reshape(tokens + FLEN, GROUPS, group_width).transpose(1, 0, 2)

    def one_group(item):
        filter_row, column = item
        kernel = jnp.where(inside, filter_row[clipped], 0.0).astype(jnp.float32)
        blocks = column.reshape(all_blocks + lag_blocks - 1, BLK, group_width)
        window = jnp.stack([blocks[lag_blocks - 1 - lag_step: lag_blocks - 1 - lag_step + all_blocks] for lag_step in range(lag_blocks)], axis=1)
        window = window.astype(jnp.float32) * live_pairs[:, :, None, None]
        return jnp.einsum("rjs,ijsw->irw", kernel, window, precision=lax.Precision.HIGHEST)

    conv = lax.map(one_group, (filters, grouped))
    conv = conv.transpose(1, 2, 0, 3).reshape(tokens, D)
    mixed = (conv + skip_bias[None, :] * gated.astype(jnp.float32)).astype(jnp.bfloat16)
    return (post_gate.astype(jnp.float32) * mixed.astype(jnp.float32)).astype(jnp.bfloat16)
```

```python
import functools

import jax
import jax.numpy as jnp
from jax import lax
from jax.experimental import pallas as pl
from jax.experimental.pallas import tpu as pltpu
from jax.sharding import PartitionSpec as P

FLEN = 4096
BLK = 128
PAIR = 2 * BLK
STEP = 4
UNITS = 8
BF = jnp.bfloat16
F32 = jnp.float32


def pack_kernel(pre_ref, val_ref, out_ref, *, quarters, width, per):
    for i in range(per):
        cols = pl.ds(i * quarters * width, quarters * width)
        gated = (pre_ref[:, cols].astype(F32) * val_ref[:, cols].astype(F32)).astype(BF)
        out_ref[:, i] = gated.T.reshape(quarters, width, BLK)


def pack(pre_gate, values, quarters, spots, width):
    rows, depth = values.shape
    per = 4
    cols = per * quarters * width
    wide = pl.BlockSpec((rows, cols), lambda i: (0, i))
    return pl.pallas_call(
        functools.partial(pack_kernel, quarters=quarters, width=width, per=per),
        grid=(spots // per,),
        in_specs=[wide, wide],
        out_specs=pl.BlockSpec((quarters, per, width, rows), lambda i: (0, i, 0, 0)),
        out_shape=jax.ShapeDtypeStruct((quarters, spots, width, rows), BF),
        name="pack",
    )(pre_gate, values)


def toeplitz_kernel(taps_ref, out_ref, *, groups, lags):
    for g in range(groups):
        for j in range(-1, 2 * lags + 1):
            if 0 <= j <= FLEN // BLK:
                window = jnp.broadcast_to(taps_ref[g : g + 1, pl.ds(j * BLK, PAIR)], (BLK, PAIR))
                turned = pltpu.roll(window, 0, 1, stride=1, stride_axis=0)
                piece = turned[:, BLK:].astype(BF)
            else:
                piece = jnp.zeros((BLK, BLK), BF)
            for half, col in ((0, 0), (1, 1), (0, 1), (1, 0)):
                if (j + half - col) % 2 == 0 and 0 <= (j + half - col) // 2 < lags:
                    row = (j + half - col) // 2 * PAIR + half * BLK
                    out_ref[g, pl.ds(row, BLK), pl.ds(col * BLK, BLK)] = piece


def toeplitz(taps, lags):
    groups = taps.shape[0]
    return pl.pallas_call(
        functools.partial(toeplitz_kernel, groups=groups, lags=lags),
        out_shape=jax.ShapeDtypeStruct((groups, lags * PAIR, PAIR), BF),
        name="toeplitz",
    )(taps)


def conv_kernel(table_ref, x_ref, w_ref, skip_ref, out_ref, acc_ref, *, groups, width, slots):
    count = table_ref[2, 0]
    last_lag = FLEN // PAIR
    last_blk = x_ref.shape[0] - 1

    def chunk(k, carry):
        places = [jnp.minimum(k * UNITS + u, count - 1) for u in range(UNITS)]
        base = [table_ref[0, p] for p in places]
        rank = [table_ref[1, p] for p in places]
        top = functools.reduce(jnp.maximum, rank)
        steps = jnp.minimum(top, last_lag) // STEP + 1
        acc_ref[...] = jnp.zeros_like(acc_ref)

        def lag_step(t, inner):
            for g in range(groups):
                rows = pl.ds(g * width, width)
                strips = []
                for u in range(UNITS):
                    parts = []
                    for i in range(STEP):
                        lag = t * STEP + i
                        live = jnp.logical_and(lag <= rank[u], lag <= last_lag)
                        first = jnp.maximum(base[u] - 2 * lag, 0)
                        second = jnp.minimum(first + 1, last_blk)
                        for b in (first, second):
                            parts.append(jnp.where(live, x_ref[b, rows, :], jnp.zeros((width, BLK), BF)))
                    strips.append(jnp.concatenate(parts, axis=1))
                left = jnp.concatenate(strips, axis=0)
                right = w_ref[g, pl.ds(pl.multiple_of(t * STEP * PAIR, STEP * PAIR), STEP * PAIR), :]
                acc_ref[g] += jnp.dot(left, right, preferred_element_type=F32)
            return inner

        lax.fori_loop(0, steps, lag_step, 0)
        for u in range(UNITS):
            second = jnp.minimum(base[u] + 1, last_blk)
            for half, b in ((1, second), (0, base[u])):
                for g in range(groups):
                    rows = pl.ds(g * width, width)
                    conv = acc_ref[g, u * width : (u + 1) * width, half * BLK : (half + 1) * BLK]
                    mixed = conv + skip_ref[rows, :] * x_ref[b, rows, :].astype(F32)
                    out_ref[b, rows, :] = mixed.astype(BF)
        return carry

    lax.fori_loop(0, (count + UNITS - 1) // UNITS, chunk, 0)


def conv(table, x, w, skip, groups, width):
    slots = table.shape[1]
    vmem = pl.BlockSpec(memory_space=pltpu.VMEM)
    return pl.pallas_call(
        functools.partial(conv_kernel, groups=groups, width=width, slots=slots),
        in_specs=[pl.BlockSpec(memory_space=pltpu.SMEM), vmem, vmem, vmem],
        out_specs=vmem,
        out_shape=jax.ShapeDtypeStruct(x.shape, BF),
        scratch_shapes=[pltpu.VMEM((groups, UNITS * width, PAIR), F32)],
        name="conv",
    )(table, x, w, skip)


def finish_kernel(mixed_ref, post_ref, out_ref, *, quarters, width, per):
    for i in range(per):
        cols = pl.ds(i * quarters * width, quarters * width)
        mixed = mixed_ref[:, i].reshape(quarters * width, BLK).T
        out_ref[:, cols] = (post_ref[:, cols].astype(F32) * mixed.astype(F32)).astype(BF)


def finish(mixed, post_gate):
    quarters, spots, width, rows = mixed.shape
    per = 4
    cols = per * quarters * width
    wide = pl.BlockSpec((rows, cols), lambda i: (0, i))
    return pl.pallas_call(
        functools.partial(finish_kernel, quarters=quarters, width=width, per=per),
        grid=(spots // per,),
        in_specs=[pl.BlockSpec((quarters, per, width, rows), lambda i: (0, i, 0, 0)), wide],
        out_specs=wide,
        out_shape=jax.ShapeDtypeStruct(post_gate.shape, BF),
        name="finish",
    )(mixed, post_gate)


def pair_table(doc_blocks, all_blocks):
    docs = doc_blocks.shape[0]
    slots = (all_blocks + docs) // 2
    pairs = (doc_blocks + 1) // 2
    earlier = jnp.arange(docs)[:, None] < jnp.arange(docs)[None, :]
    doc_first = jnp.sum(jnp.where(earlier, doc_blocks[:, None], 0), axis=0)
    pair_first = jnp.sum(jnp.where(earlier, pairs[:, None], 0), axis=0)
    slot = jnp.arange(slots, dtype=jnp.int32)[:, None]
    mine = (slot >= pair_first[None, :]) & (slot < (pair_first + pairs)[None, :])
    rank = slot - pair_first[None, :]
    base = jnp.sum(jnp.where(mine, doc_first[None, :] + 2 * rank, 0), axis=1)
    rank = jnp.sum(jnp.where(mine, rank, 0), axis=1)
    count = jnp.broadcast_to(jnp.sum(pairs), (slots,))
    return jnp.stack([base, rank, count]).astype(jnp.int32)


def per_device(post_gate, pre_gate, values, filters, skip_bias, doc_blocks):
    quarters, spots = lax.axis_size("stretch"), lax.axis_size("ctx")
    devices = quarters * spots
    width = values.shape[1] // devices
    groups = filters.shape[0] // quarters
    group_width = width // groups
    both = ("stretch", "ctx")
    packed = pack(pre_gate, values, quarters, spots, width)
    x = lax.all_to_all(packed.reshape(devices, width, BLK), both, 0, 0)
    mine = lax.axis_index("stretch")
    taps = lax.dynamic_slice_in_dim(filters, mine * groups, groups, 0)
    taps = jnp.pad(taps, ((0, 0), (BLK, BLK)))
    lags = -(-(FLEN // PAIR + 1) // STEP) * STEP
    w = toeplitz(taps, lags)
    skip = lax.dynamic_slice_in_dim(skip_bias, mine * width, width, 0)
    skip = jnp.broadcast_to(skip[:, None], (width, BLK))
    table = pair_table(doc_blocks, devices)
    mixed = conv(table, x, w, skip, groups, group_width)
    back = lax.all_to_all(mixed, both, 0, 0)
    return finish(back.reshape(quarters, spots, width, BLK), post_gate)


def solution(mesh):
    in_specs = (
        P(("stretch", "ctx"), None),
        P(("stretch", "ctx"), None),
        P(("stretch", "ctx"), None),
        P("ctx", None),
        P("ctx"),
        P(),
    )
    return jax.shard_map(
        per_device, mesh=mesh, in_specs=in_specs, out_specs=P(("stretch", "ctx"), None), check_vma=False
    )
```

```python
import functools

import jax
import jax.numpy as jnp
from jax import lax
from jax.experimental import pallas as pl
from jax.experimental.pallas import tpu as pltpu
from jax.sharding import PartitionSpec as P

FLEN = 4096
BLK = 128
PAIR = 2 * BLK
STEP = 4
UNITS = 8
VMEM_LIMIT = 16 << 20
BF = jnp.bfloat16
F32 = jnp.float32


def resident(x):
    return pltpu.with_memory_space_constraint(x, pltpu.VMEM)


def distant(x):
    return pltpu.with_memory_space_constraint(x, pltpu.HBM)


def pack_kernel(pre_ref, val_ref, out_ref, pre_buf, val_buf, out_buf, sems, *, pieces):
    quarters, spots, width, rows = out_ref.shape
    per = spots // pieces
    cols = per * quarters * width
    copies = []
    for k in range(pieces):
        part = pl.ds(k * cols, cols)
        pair = [
            pltpu.make_async_copy(src.at[:, part], dst.at[:, part], sems.at[k, i])
            for i, (src, dst) in enumerate(((pre_ref, pre_buf), (val_ref, val_buf)))
        ]
        for copy in pair:
            copy.start()
        copies.append(pair)
    for k in range(pieces):
        for copy in copies[k]:
            copy.wait()
        for i in range(k * per, (k + 1) * per):
            part = pl.ds(i * quarters * width, quarters * width)
            gated = (pre_buf[:, part].astype(F32) * val_buf[:, part].astype(F32)).astype(BF)
            out_buf[:, i] = gated.T.reshape(quarters, width, rows)
        part = pl.ds(k * per, per)
        copy = pltpu.make_async_copy(out_buf.at[:, part], out_ref.at[:, part], sems.at[k, 2])
        copy.start()
        copies[k] = [copy]
    for (copy,) in copies:
        copy.wait()


def pack(pre_gate, values, quarters, spots, width):
    rows, depth = values.shape
    pieces = 8
    whole = pl.BlockSpec(memory_space=pltpu.HBM)
    return pl.pallas_call(
        functools.partial(pack_kernel, pieces=pieces),
        in_specs=[whole, whole],
        out_specs=whole,
        out_shape=jax.ShapeDtypeStruct((quarters, spots, width, rows), BF),
        scratch_shapes=[
            pltpu.VMEM((rows, depth), BF),
            pltpu.VMEM((rows, depth), BF),
            pltpu.VMEM((quarters, spots, width, rows), BF),
            pltpu.SemaphoreType.DMA((pieces, 3)),
        ],
        compiler_params=pltpu.CompilerParams(vmem_limit_bytes=VMEM_LIMIT),
        name="pack",
    )(distant(pre_gate), distant(values))


def toeplitz_kernel(taps_ref, bias_ref, out_ref, skip_ref):
    groups, tiles = out_ref.shape[:2]
    for g in range(groups):
        for k in range(tiles):
            if 1 <= k <= FLEN // BLK + 1:
                taps = taps_ref[g : g + 1, pl.ds((k - 1) * BLK, PAIR)]
                window = jnp.broadcast_to(taps, (BLK, PAIR))
                turned = pltpu.roll(window, 0, 1, stride=1, stride_axis=0)
                out_ref[g, k] = turned[:, BLK:].astype(BF)
            else:
                out_ref[g, k] = jnp.zeros((BLK, BLK), BF)
    skip_ref[...] = jnp.broadcast_to(bias_ref[...], (BLK, BLK)).T[: skip_ref.shape[0]]


def toeplitz(taps, bias):
    groups = taps.shape[0]
    steps = FLEN // PAIR // STEP + 1
    width = bias.shape[0]
    return pl.pallas_call(
        toeplitz_kernel,
        out_shape=[
            jax.ShapeDtypeStruct((groups, 2 * steps * STEP + 1, BLK, BLK), BF),
            jax.ShapeDtypeStruct((width, BLK), F32),
        ],
        compiler_params=pltpu.CompilerParams(vmem_limit_bytes=VMEM_LIMIT),
        name="toeplitz",
    )(taps, jnp.pad(bias, (0, BLK - width))[None, :])


def conv_kernel(table_ref, x_ref, tiles_hbm, skip_hbm, out_ref, tiles_ref, skip_ref, acc_ref, sems, *, width):
    groups = tiles_ref.shape[0]
    count = table_ref[2, 0]
    last_lag = FLEN // PAIR
    last_blk = x_ref.shape[0] - 1
    early = 2 * STEP + 1
    loads = [
        pltpu.make_async_copy(tiles_hbm.at[:, :early], tiles_ref.at[:, :early], sems.at[0]),
        pltpu.make_async_copy(skip_hbm, skip_ref, sems.at[1]),
        pltpu.make_async_copy(tiles_hbm.at[:, early:], tiles_ref.at[:, early:], sems.at[2]),
    ]
    for load in loads:
        load.start()
    for load in loads:
        load.wait()

    def chunk(k, carry):
        places = [jnp.minimum(k * UNITS + u, count - 1) for u in range(UNITS)]
        base = [table_ref[0, p] for p in places]
        rank = [table_ref[1, p] for p in places]
        top = functools.reduce(jnp.maximum, rank)
        steps = jnp.minimum(top, last_lag) // STEP + 1
        acc_ref[...] = jnp.zeros_like(acc_ref)

        def lag_step(t, inner):
            for g in range(groups):
                rows = pl.ds(g * width, width)
                strips = []
                for u in range(UNITS):
                    parts = []
                    for i in range(STEP):
                        lag = t * STEP + i
                        live = jnp.logical_and(lag <= rank[u], lag <= last_lag)
                        first = jnp.maximum(base[u] - 2 * lag, 0)
                        second = jnp.minimum(first + 1, last_blk)
                        for b in (first, second):
                            parts.append(jnp.where(live, x_ref[b, rows, :], jnp.zeros((width, BLK), BF)))
                    strips.append(jnp.concatenate(parts, axis=1))
                left = jnp.concatenate(strips, axis=0)
                right = []
                for i in range(STEP):
                    k = 2 * (t * STEP + i) + 1
                    right.append(jnp.concatenate([tiles_ref[g, k], tiles_ref[g, k + 1]], axis=1))
                    right.append(jnp.concatenate([tiles_ref[g, k - 1], tiles_ref[g, k]], axis=1))
                right = jnp.concatenate(right, axis=0)
                acc_ref[g] += jnp.dot(left, right, preferred_element_type=F32)
            return inner

        lax.fori_loop(0, steps, lag_step, 0)
        for u in range(UNITS):
            second = jnp.minimum(base[u] + 1, last_blk)
            for half, b in ((1, second), (0, base[u])):
                for g in range(groups):
                    rows = pl.ds(g * width, width)
                    total = acc_ref[g, u * width : (u + 1) * width, half * BLK : (half + 1) * BLK]
                    mixed = total + skip_ref[rows, :] * x_ref[b, rows, :].astype(F32)
                    out_ref[b, rows, :] = mixed.astype(BF)
        return carry

    lax.fori_loop(0, (count + UNITS - 1) // UNITS, chunk, 0)


def conv(table, x, tiles, skip, width):
    vmem = pl.BlockSpec(memory_space=pltpu.VMEM)
    hbm = pl.BlockSpec(memory_space=pltpu.HBM)
    return pl.pallas_call(
        functools.partial(conv_kernel, width=width),
        in_specs=[pl.BlockSpec(memory_space=pltpu.SMEM), vmem, hbm, hbm],
        out_specs=vmem,
        out_shape=pltpu.VMEM(x.shape, BF),
        scratch_shapes=[
            pltpu.VMEM(tiles.shape, BF),
            pltpu.VMEM(skip.shape, F32),
            pltpu.VMEM((tiles.shape[0], UNITS * width, PAIR), F32),
            pltpu.SemaphoreType.DMA((3,)),
        ],
        compiler_params=pltpu.CompilerParams(vmem_limit_bytes=VMEM_LIMIT),
        name="conv",
    )(table, resident(x), distant(tiles), distant(skip))


def finish_kernel(mixed_ref, post_ref, out_ref, buf, sems, *, pieces):
    quarters, spots, width, rows = mixed_ref.shape
    per = spots // pieces
    cols = per * quarters * width
    copies = []
    for k in range(pieces):
        for i in range(k * per, (k + 1) * per):
            part = pl.ds(i * quarters * width, quarters * width)
            mixed = mixed_ref[:, i].reshape(quarters * width, rows).T
            buf[:, part] = (post_ref[:, part].astype(F32) * mixed.astype(F32)).astype(BF)
        part = pl.ds(k * cols, cols)
        copy = pltpu.make_async_copy(buf.at[:, part], out_ref.at[:, part], sems.at[k])
        copy.start()
        copies.append(copy)
    for copy in copies:
        copy.wait()


def finish(mixed, post_gate):
    pieces = 8
    vmem = pl.BlockSpec(memory_space=pltpu.VMEM)
    return pl.pallas_call(
        functools.partial(finish_kernel, pieces=pieces),
        in_specs=[vmem, vmem],
        out_specs=pl.BlockSpec(memory_space=pltpu.HBM),
        out_shape=jax.ShapeDtypeStruct(post_gate.shape, BF),
        scratch_shapes=[pltpu.VMEM(post_gate.shape, BF), pltpu.SemaphoreType.DMA((pieces,))],
        compiler_params=pltpu.CompilerParams(vmem_limit_bytes=VMEM_LIMIT),
        name="finish",
    )(resident(mixed), resident(post_gate))


def pair_table(doc_blocks, all_blocks):
    docs = doc_blocks.shape[0]
    slots = (all_blocks + docs) // 2
    pairs = (doc_blocks + 1) // 2
    earlier = jnp.arange(docs)[:, None] < jnp.arange(docs)[None, :]
    doc_first = jnp.sum(jnp.where(earlier, doc_blocks[:, None], 0), axis=0)
    pair_first = jnp.sum(jnp.where(earlier, pairs[:, None], 0), axis=0)
    slot = jnp.arange(slots, dtype=jnp.int32)[:, None]
    mine = (slot >= pair_first[None, :]) & (slot < (pair_first + pairs)[None, :])
    rank = slot - pair_first[None, :]
    base = jnp.sum(jnp.where(mine, doc_first[None, :] + 2 * rank, 0), axis=1)
    rank = jnp.sum(jnp.where(mine, rank, 0), axis=1)
    count = jnp.broadcast_to(jnp.sum(pairs), (slots,))
    return jnp.stack([base, rank, count]).astype(jnp.int32)


def per_device(post_gate, pre_gate, values, filters, skip_bias, doc_blocks):
    quarters, spots = lax.axis_size("stretch"), lax.axis_size("ctx")
    devices = quarters * spots
    width = values.shape[1] // devices
    groups = filters.shape[0] // quarters
    group_width = width // groups
    both = ("stretch", "ctx")
    packed = pack(pre_gate, values, quarters, spots, width)
    x = lax.all_to_all(packed.reshape(devices, width, BLK), both, 0, 0)
    mine = lax.axis_index("stretch")
    taps = lax.dynamic_slice_in_dim(filters, mine * groups, groups, 0)
    taps = jnp.pad(taps, ((0, 0), (BLK, BLK)))
    skip = lax.dynamic_slice_in_dim(skip_bias, mine * width, width, 0)
    tiles, skip = toeplitz(taps, skip)
    table = pair_table(doc_blocks, devices)
    mixed = conv(table, x, tiles, skip, group_width)
    back = lax.all_to_all(mixed, both, 0, 0)
    return finish(back.reshape(quarters, spots, width, BLK), post_gate)


def solution(mesh):
    in_specs = (
        P(("stretch", "ctx"), None),
        P(("stretch", "ctx"), None),
        P(("stretch", "ctx"), None),
        P("ctx", None),
        P("ctx"),
        P(),
    )
    return jax.shard_map(
        per_device, mesh=mesh, in_specs=in_specs, out_specs=P(("stretch", "ctx"), None), check_vma=False
    )
```

```python
import functools

import jax
import jax.numpy as jnp
from jax import lax
from jax.experimental import pallas as pl
from jax.experimental.pallas import tpu as pltpu
from jax.sharding import PartitionSpec as P

FLEN = 4096
BLK = 128
PAIR = 2 * BLK
LIGHT = 4
HEAVY = 6
UNITS = 8
VMEM_LIMIT = 16 << 20
BF = jnp.bfloat16
F32 = jnp.float32


def resident(x):
    return pltpu.with_memory_space_constraint(x, pltpu.VMEM)


def distant(x):
    return pltpu.with_memory_space_constraint(x, pltpu.HBM)


def pack_kernel(pre_ref, val_ref, out_ref, pre_buf, val_buf, out_buf, sems, *, pieces):
    quarters, spots, width, rows = out_ref.shape
    per = spots // pieces
    cols = per * quarters * width
    copies = []
    for k in range(pieces):
        part = pl.ds(k * cols, cols)
        pair = [
            pltpu.make_async_copy(src.at[:, part], dst.at[:, part], sems.at[k, i])
            for i, (src, dst) in enumerate(((pre_ref, pre_buf), (val_ref, val_buf)))
        ]
        for copy in pair:
            copy.start()
        copies.append(pair)
    for k in range(pieces):
        for copy in copies[k]:
            copy.wait()
        for i in range(k * per, (k + 1) * per):
            part = pl.ds(i * quarters * width, quarters * width)
            gated = (pre_buf[:, part].astype(F32) * val_buf[:, part].astype(F32)).astype(BF)
            out_buf[:, i] = gated.T.reshape(quarters, width, rows)
        part = pl.ds(k * per, per)
        copy = pltpu.make_async_copy(out_buf.at[:, part], out_ref.at[:, part], sems.at[k, 2])
        copy.start()
        copies[k] = [copy]
    for (copy,) in copies:
        copy.wait()


def pack(pre_gate, values, quarters, spots, width):
    rows, depth = values.shape
    pieces = 8
    whole = pl.BlockSpec(memory_space=pltpu.HBM)
    return pl.pallas_call(
        functools.partial(pack_kernel, pieces=pieces),
        in_specs=[whole, whole],
        out_specs=whole,
        out_shape=jax.ShapeDtypeStruct((quarters, spots, width, rows), BF),
        scratch_shapes=[
            pltpu.VMEM((rows, depth), BF),
            pltpu.VMEM((rows, depth), BF),
            pltpu.VMEM((quarters, spots, width, rows), BF),
            pltpu.SemaphoreType.DMA((pieces, 3)),
        ],
        compiler_params=pltpu.CompilerParams(vmem_limit_bytes=VMEM_LIMIT),
        name="pack",
    )(distant(pre_gate), distant(values))


def toeplitz_kernel(taps_ref, bias_ref, out_ref, near_ref, skip_ref):
    groups, tiles = out_ref.shape[:2]
    for g in range(groups):
        for k in range(tiles):
            if 1 <= k <= FLEN // BLK + 1:
                taps = taps_ref[g : g + 1, pl.ds((k - 1) * BLK, PAIR)]
                window = jnp.broadcast_to(taps, (BLK, PAIR))
                turned = pltpu.roll(window, 0, 1, stride=1, stride_axis=0)
                tile = turned[:, BLK:].astype(BF)
            else:
                tile = jnp.zeros((BLK, BLK), BF)
            out_ref[g, k] = tile
            if k < near_ref.shape[1]:
                near_ref[g, k] = tile
    skip_ref[...] = jnp.broadcast_to(bias_ref[...], (BLK, BLK)).T[: skip_ref.shape[0]]


def toeplitz(taps, bias):
    groups = taps.shape[0]
    width = bias.shape[0]
    return pl.pallas_call(
        toeplitz_kernel,
        out_shape=[
            jax.ShapeDtypeStruct((groups, FLEN // BLK + 3, BLK, BLK), BF),
            pltpu.VMEM((groups, 2 * LIGHT + 1, BLK, BLK), BF),
            pltpu.VMEM((width, BLK), F32),
        ],
        compiler_params=pltpu.CompilerParams(vmem_limit_bytes=VMEM_LIMIT),
        name="toeplitz",
    )(taps, jnp.pad(bias, (0, BLK - width))[None, :])


def conv_kernel(table_ref, x_ref, near_ref, skip_ref, tiles_hbm, out_ref, tiles_ref, acc_ref, sem, *, width):
    groups = tiles_ref.shape[0]
    count, light = table_ref[3, 0], table_ref[4, 0]
    chunks = (count + UNITS - 1) // UNITS
    last_lag = FLEN // PAIR
    last_blk = x_ref.shape[0] - 1
    load = pltpu.make_async_copy(tiles_hbm, tiles_ref, sem)
    load.start()

    def product(weights_ref, g, base, rank, start, lags):
        rows = pl.ds(g * width, width)
        zeros = jnp.zeros((width, BLK), BF)
        strips = []
        for u in range(UNITS):
            parts = []
            for i in range(lags):
                live = start + i <= rank[u]
                before = jnp.maximum(base[u] - 2 * (start + i), 0)
                after = jnp.minimum(before + 1, last_blk)
                for b in (before, after):
                    parts.append(jnp.where(live, x_ref[b, rows, :], zeros))
            strips.append(jnp.concatenate(parts, axis=1))
        left = jnp.concatenate(strips, axis=0)
        right = []
        for i in range(lags):
            k = 2 * (start + i) + 1
            right.append(jnp.concatenate([weights_ref[g, k], weights_ref[g, k + 1]], axis=1))
            right.append(jnp.concatenate([weights_ref[g, k - 1], weights_ref[g, k]], axis=1))
        right = jnp.concatenate(right, axis=0)
        return jnp.dot(left, right, preferred_element_type=F32)

    def store(g, total, base, second):
        rows = pl.ds(g * width, width)
        for u in range(UNITS):
            for half, b in ((1, second[u]), (0, base[u])):
                part = total[u * width : (u + 1) * width, half * BLK : (half + 1) * BLK]
                mixed = part + skip_ref[rows, :] * x_ref[b, rows, :].astype(F32)
                out_ref[b, rows, :] = mixed.astype(BF)

    def entries(k):
        places = [jnp.minimum(k * UNITS + u, count - 1) for u in range(UNITS)]
        return [[table_ref[row, p] for p in places] for row in range(3)]

    def light_chunk(k, carry):
        base, second, rank = entries(k)
        for size in range(1, LIGHT + 1):

            @pl.when(rank[-1] + 1 == size)
            def _(size=size):
                for g in range(groups):
                    store(g, product(near_ref, g, base, rank, 0, size), base, second)

        return carry

    def heavy_chunk(k, carry):
        base, second, rank = entries(k)
        lags = jnp.minimum(rank[-1], last_lag) + 1
        whole = (lags - 1) // HEAVY
        acc_ref[...] = jnp.zeros_like(acc_ref)

        def lag_step(t, inner):
            for g in range(groups):
                acc_ref[g] += product(tiles_ref, g, base, rank, t * HEAVY, HEAVY)
            return inner

        lax.fori_loop(0, whole, lag_step, 0)
        for size in range(1, HEAVY + 1):

            @pl.when(lags - whole * HEAVY == size)
            def _(size=size):
                for g in range(groups):
                    total = acc_ref[g] + product(tiles_ref, g, base, rank, whole * HEAVY, size)
                    store(g, total, base, second)

        return carry

    lax.fori_loop(0, light, light_chunk, 0)
    load.wait()
    lax.fori_loop(light, chunks, heavy_chunk, 0)


def conv(table, x, near, skip, tiles, width):
    vmem = pl.BlockSpec(memory_space=pltpu.VMEM)
    hbm = pl.BlockSpec(memory_space=pltpu.HBM)
    return pl.pallas_call(
        functools.partial(conv_kernel, width=width),
        in_specs=[pl.BlockSpec(memory_space=pltpu.SMEM), vmem, vmem, vmem, hbm],
        out_specs=vmem,
        out_shape=pltpu.VMEM(x.shape, BF),
        scratch_shapes=[
            pltpu.VMEM(tiles.shape, BF),
            pltpu.VMEM((tiles.shape[0], UNITS * width, PAIR), F32),
            pltpu.SemaphoreType.DMA,
        ],
        compiler_params=pltpu.CompilerParams(vmem_limit_bytes=VMEM_LIMIT),
        name="conv",
    )(table, resident(x), resident(near), resident(skip), distant(tiles))


def finish_kernel(mixed_ref, post_ref, out_ref, buf, sems, *, pieces):
    quarters, spots, width, rows = mixed_ref.shape
    per = spots // pieces
    cols = per * quarters * width
    copies = []
    for k in range(pieces):
        for i in range(k * per, (k + 1) * per):
            part = pl.ds(i * quarters * width, quarters * width)
            mixed = mixed_ref[:, i].reshape(quarters * width, rows).T
            buf[:, part] = (post_ref[:, part].astype(F32) * mixed.astype(F32)).astype(BF)
        part = pl.ds(k * cols, cols)
        copy = pltpu.make_async_copy(buf.at[:, part], out_ref.at[:, part], sems.at[k])
        copy.start()
        copies.append(copy)
    for copy in copies:
        copy.wait()


def finish(mixed, post_gate):
    pieces = 8
    vmem = pl.BlockSpec(memory_space=pltpu.VMEM)
    return pl.pallas_call(
        functools.partial(finish_kernel, pieces=pieces),
        in_specs=[vmem, vmem],
        out_specs=pl.BlockSpec(memory_space=pltpu.HBM),
        out_shape=jax.ShapeDtypeStruct(post_gate.shape, BF),
        scratch_shapes=[pltpu.VMEM(post_gate.shape, BF), pltpu.SemaphoreType.DMA((pieces,))],
        compiler_params=pltpu.CompilerParams(vmem_limit_bytes=VMEM_LIMIT),
        name="finish",
    )(resident(mixed), resident(post_gate))


def pair_table(doc_blocks, all_blocks):
    docs = doc_blocks.shape[0]
    slots = (all_blocks + docs) // 2
    pairs = (doc_blocks + 1) // 2
    earlier = jnp.arange(docs)[:, None] < jnp.arange(docs)[None, :]
    doc_first = jnp.sum(jnp.where(earlier, doc_blocks[:, None], 0), axis=0)
    pair_first = jnp.sum(jnp.where(earlier, pairs[:, None], 0), axis=0)
    count = jnp.sum(pairs)
    slot = jnp.arange(slots, dtype=jnp.int32)
    mine = (slot[:, None] >= pair_first[None, :]) & (slot[:, None] < (pair_first + pairs)[None, :])
    place = slot[:, None] - pair_first[None, :]
    rank = jnp.sum(jnp.where(mine, place, 0), axis=1) + jnp.where(slot < count, 0, slots)
    base = jnp.sum(jnp.where(mine, doc_first[None, :] + 2 * place, 0), axis=1)
    both = jnp.sum(jnp.where(mine & (2 * place + 1 < doc_blocks[None, :]), 1, 0), axis=1)
    key = rank * slots + slot
    order = jnp.sum((key[None, :] < key[:, None]).astype(jnp.int32), axis=1)
    moved = order[None, :] == slot[:, None]
    columns = [jnp.sum(jnp.where(moved, c[None, :], 0), axis=1) for c in (base, base + both, rank)]
    light = jnp.sum((rank < LIGHT).astype(jnp.int32)) // UNITS
    return jnp.stack(columns + [jnp.full((slots,), count), jnp.full((slots,), light)]).astype(jnp.int32)


def per_device(post_gate, pre_gate, values, filters, skip_bias, doc_blocks):
    quarters, spots = lax.axis_size("stretch"), lax.axis_size("ctx")
    devices = quarters * spots
    width = values.shape[1] // devices
    groups = filters.shape[0] // quarters
    group_width = width // groups
    both = ("stretch", "ctx")
    packed = pack(pre_gate, values, quarters, spots, width)
    x = lax.all_to_all(packed.reshape(devices, width, BLK), both, 0, 0)
    mine = lax.axis_index("stretch")
    taps = lax.dynamic_slice_in_dim(filters, mine * groups, groups, 0)
    taps = jnp.pad(taps, ((0, 0), (BLK, BLK)))
    skip = lax.dynamic_slice_in_dim(skip_bias, mine * width, width, 0)
    tiles, near, skip = toeplitz(taps, skip)
    table = pair_table(doc_blocks, devices)
    mixed = conv(table, x, near, skip, tiles, group_width)
    back = lax.all_to_all(mixed, both, 0, 0)
    return finish(back.reshape(quarters, spots, width, BLK), post_gate)


def solution(mesh):
    in_specs = (
        P(("stretch", "ctx"), None),
        P(("stretch", "ctx"), None),
        P(("stretch", "ctx"), None),
        P("ctx", None),
        P("ctx"),
        P(),
    )
    return jax.shard_map(
        per_device, mesh=mesh, in_specs=in_specs, out_specs=P(("stretch", "ctx"), None), check_vma=False
    )
```

```python
import functools

import jax
import jax.numpy as jnp
from jax import lax
from jax.experimental import pallas as pl
from jax.experimental.pallas import tpu as pltpu
from jax.sharding import PartitionSpec as P

FLEN = 4096
BLK = 128
PAIR = 2 * BLK
LIGHT = 4
HEAVY = 6
UNITS = 8
VMEM_LIMIT = 16 << 20
BF = jnp.bfloat16
F32 = jnp.float32


def resident(x):
    return pltpu.with_memory_space_constraint(x, pltpu.VMEM)


def distant(x):
    return pltpu.with_memory_space_constraint(x, pltpu.HBM)


def pack_kernel(pre_ref, val_ref, out_ref, pre_buf, val_buf, out_buf, sems, *, pieces):
    quarters, spots, width, rows = out_ref.shape
    per = spots // pieces
    cols = per * quarters * width
    copies = []
    for k in range(pieces):
        part = pl.ds(k * cols, cols)
        pair = [
            pltpu.make_async_copy(src.at[:, part], dst.at[:, part], sems.at[k, i])
            for i, (src, dst) in enumerate(((pre_ref, pre_buf), (val_ref, val_buf)))
        ]
        for copy in pair:
            copy.start()
        copies.append(pair)
    for k in range(pieces):
        for copy in copies[k]:
            copy.wait()
        for i in range(k * per, (k + 1) * per):
            part = pl.ds(i * quarters * width, quarters * width)
            gated = (pre_buf[:, part].astype(F32) * val_buf[:, part].astype(F32)).astype(BF)
            out_buf[:, i] = gated.T.reshape(quarters, width, rows)
        part = pl.ds(k * per, per)
        copy = pltpu.make_async_copy(out_buf.at[:, part], out_ref.at[:, part], sems.at[k, 2])
        copy.start()
        copies[k] = [copy]
    for (copy,) in copies:
        copy.wait()


def pack(pre_gate, values, quarters, spots, width):
    rows, depth = values.shape
    pieces = 4
    whole = pl.BlockSpec(memory_space=pltpu.HBM)
    return pl.pallas_call(
        functools.partial(pack_kernel, pieces=pieces),
        in_specs=[whole, whole],
        out_specs=whole,
        out_shape=pltpu.HBM((quarters, spots, width, rows), BF),
        scratch_shapes=[
            pltpu.VMEM((rows, depth), BF),
            pltpu.VMEM((rows, depth), BF),
            pltpu.VMEM((quarters, spots, width, rows), BF),
            pltpu.SemaphoreType.DMA((pieces, 3)),
        ],
        compiler_params=pltpu.CompilerParams(vmem_limit_bytes=VMEM_LIMIT),
        name="pack",
    )(distant(pre_gate), distant(values))


def toeplitz_kernel(taps_ref, bias_ref, out_ref, near_ref, skip_ref):
    groups, tiles = out_ref.shape[:2]
    for g in range(groups):
        for k in range(tiles):
            if 1 <= k <= FLEN // BLK + 1:
                taps = taps_ref[g : g + 1, pl.ds((k - 1) * BLK, PAIR)]
                window = jnp.broadcast_to(taps, (BLK, PAIR))
                turned = pltpu.roll(window, 0, 1, stride=1, stride_axis=0)
                tile = turned[:, BLK:].astype(BF)
            else:
                tile = jnp.zeros((BLK, BLK), BF)
            out_ref[g, k] = tile
            if k < near_ref.shape[1]:
                near_ref[g, k] = tile
    skip_ref[...] = jnp.broadcast_to(bias_ref[...], (BLK, BLK)).T[: skip_ref.shape[0]]


def toeplitz(taps, bias):
    groups = taps.shape[0]
    width = bias.shape[0]
    return pl.pallas_call(
        toeplitz_kernel,
        out_shape=[
            jax.ShapeDtypeStruct((groups, FLEN // BLK + 3, BLK, BLK), BF),
            pltpu.VMEM((groups, 2 * LIGHT + 1, BLK, BLK), BF),
            pltpu.VMEM((width, BLK), F32),
        ],
        compiler_params=pltpu.CompilerParams(vmem_limit_bytes=VMEM_LIMIT),
        name="toeplitz",
    )(taps, jnp.pad(bias, (0, BLK - width))[None, :])


def conv_kernel(table_ref, x_ref, near_ref, skip_ref, tiles_hbm, out_ref, tiles_ref, acc_ref, sem, *, width):
    groups = tiles_ref.shape[0]
    count, light = table_ref[3, 0], table_ref[4, 0]
    chunks = (count + UNITS - 1) // UNITS
    spare = chunks * UNITS - count
    last_lag = FLEN // PAIR
    last_blk = x_ref.shape[0] - 1
    load = pltpu.make_async_copy(tiles_hbm, tiles_ref, sem)
    load.start()

    def product(weights_ref, g, base, rank, start, lags):
        rows = pl.ds(g * width, width)
        zeros = jnp.zeros((width, BLK), BF)
        strips = []
        for u in range(UNITS):
            parts = []
            for i in range(lags):
                live = start + i <= rank[u]
                before = jnp.maximum(base[u] - 2 * (start + i), 0)
                after = jnp.minimum(before + 1, last_blk)
                for b in (before, after):
                    parts.append(jnp.where(live, x_ref[b, rows, :], zeros))
            strips.append(jnp.concatenate(parts, axis=1))
        left = jnp.concatenate(strips, axis=0)
        right = []
        for i in range(lags):
            k = 2 * (start + i) + 1
            right.append(jnp.concatenate([weights_ref[g, k], weights_ref[g, k + 1]], axis=1))
            right.append(jnp.concatenate([weights_ref[g, k - 1], weights_ref[g, k]], axis=1))
        right = jnp.concatenate(right, axis=0)
        return jnp.dot(left, right, preferred_element_type=F32)

    def store(g, total, base, second):
        rows = pl.ds(g * width, width)
        for u in range(UNITS):
            for half, b in ((1, second[u]), (0, base[u])):
                part = total[u * width : (u + 1) * width, half * BLK : (half + 1) * BLK]
                mixed = part + skip_ref[rows, :] * x_ref[b, rows, :].astype(F32)
                out_ref[b, rows, :] = mixed.astype(BF)

    def entries(k):
        places = [jnp.maximum(k * UNITS + u - spare, 0) for u in range(UNITS)]
        return [[table_ref[row, p] for p in places] for row in range(3)]

    def light_chunk(k, carry):
        base, second, rank = entries(k)
        for size in range(1, LIGHT + 1):

            @pl.when(rank[-1] + 1 == size)
            def _(size=size):
                for g in range(groups):
                    store(g, product(near_ref, g, base, rank, 0, size), base, second)

        return carry

    def heavy_chunk(k, carry):
        base, second, rank = entries(k)
        lags = jnp.minimum(rank[-1], last_lag) + 1
        whole = (lags - 1) // HEAVY
        acc_ref[...] = jnp.zeros_like(acc_ref)

        def lag_step(t, inner):
            for g in range(groups):
                acc_ref[g] += product(tiles_ref, g, base, rank, t * HEAVY, HEAVY)
            return inner

        lax.fori_loop(0, whole, lag_step, 0)
        for size in range(1, HEAVY + 1):

            @pl.when(lags - whole * HEAVY == size)
            def _(size=size):
                for g in range(groups):
                    total = acc_ref[g] + product(tiles_ref, g, base, rank, whole * HEAVY, size)
                    store(g, total, base, second)

        return carry

    lax.fori_loop(0, light, light_chunk, 0)
    load.wait()
    lax.fori_loop(light, chunks, heavy_chunk, 0)


def conv(table, x, near, skip, tiles, width):
    vmem = pl.BlockSpec(memory_space=pltpu.VMEM)
    hbm = pl.BlockSpec(memory_space=pltpu.HBM)
    return pl.pallas_call(
        functools.partial(conv_kernel, width=width),
        in_specs=[pl.BlockSpec(memory_space=pltpu.SMEM), vmem, vmem, vmem, hbm],
        out_specs=vmem,
        out_shape=pltpu.VMEM(x.shape, BF),
        scratch_shapes=[
            pltpu.VMEM(tiles.shape, BF),
            pltpu.VMEM((tiles.shape[0], UNITS * width, PAIR), F32),
            pltpu.SemaphoreType.DMA,
        ],
        compiler_params=pltpu.CompilerParams(vmem_limit_bytes=VMEM_LIMIT),
        name="conv",
    )(table, resident(x), resident(near), resident(skip), distant(tiles))


def finish_kernel(mixed_ref, post_ref, out_ref, buf, sems, *, pieces):
    quarters, spots, width, rows = mixed_ref.shape
    per = spots // pieces
    cols = per * quarters * width
    copies = []
    for k in range(pieces):
        for i in range(k * per, (k + 1) * per):
            part = pl.ds(i * quarters * width, quarters * width)
            mixed = mixed_ref[:, i].reshape(quarters * width, rows).T
            buf[:, part] = (post_ref[:, part].astype(F32) * mixed.astype(F32)).astype(BF)
        part = pl.ds(k * cols, cols)
        copy = pltpu.make_async_copy(buf.at[:, part], out_ref.at[:, part], sems.at[k])
        copy.start()
        copies.append(copy)
    for copy in copies:
        copy.wait()


def finish(mixed, post_gate):
    pieces = 8
    vmem = pl.BlockSpec(memory_space=pltpu.VMEM)
    return pl.pallas_call(
        functools.partial(finish_kernel, pieces=pieces),
        in_specs=[vmem, vmem],
        out_specs=pl.BlockSpec(memory_space=pltpu.HBM),
        out_shape=jax.ShapeDtypeStruct(post_gate.shape, BF),
        scratch_shapes=[pltpu.VMEM(post_gate.shape, BF), pltpu.SemaphoreType.DMA((pieces,))],
        compiler_params=pltpu.CompilerParams(vmem_limit_bytes=VMEM_LIMIT),
        name="finish",
    )(resident(mixed), resident(post_gate))


def pair_table(doc_blocks, all_blocks):
    docs = doc_blocks.shape[0]
    slots = (all_blocks + docs) // 2
    pairs = (doc_blocks + 1) // 2
    earlier = jnp.arange(docs)[:, None] < jnp.arange(docs)[None, :]
    doc_first = jnp.sum(jnp.where(earlier, doc_blocks[:, None], 0), axis=0)
    pair_first = jnp.sum(jnp.where(earlier, pairs[:, None], 0), axis=0)
    count = jnp.sum(pairs)
    slot = jnp.arange(slots, dtype=jnp.int32)
    mine = (slot[:, None] >= pair_first[None, :]) & (slot[:, None] < (pair_first + pairs)[None, :])
    place = slot[:, None] - pair_first[None, :]
    rank = jnp.sum(jnp.where(mine, place, 0), axis=1) + jnp.where(slot < count, 0, slots)
    base = jnp.sum(jnp.where(mine, doc_first[None, :] + 2 * place, 0), axis=1)
    both = jnp.sum(jnp.where(mine & (2 * place + 1 < doc_blocks[None, :]), 1, 0), axis=1)
    key = rank * slots + slot
    order = jnp.sum((key[None, :] < key[:, None]).astype(jnp.int32), axis=1)
    moved = order[None, :] == slot[:, None]
    columns = [jnp.sum(jnp.where(moved, c[None, :], 0), axis=1) for c in (base, base + both, rank)]
    light = (jnp.sum((rank < LIGHT).astype(jnp.int32)) + (-count) % UNITS) // UNITS
    return jnp.stack(columns + [jnp.full((slots,), count), jnp.full((slots,), light)]).astype(jnp.int32)


def per_device(post_gate, pre_gate, values, filters, skip_bias, doc_blocks):
    quarters, spots = lax.axis_size("stretch"), lax.axis_size("ctx")
    devices = quarters * spots
    width = values.shape[1] // devices
    groups = filters.shape[0] // quarters
    group_width = width // groups
    both = ("stretch", "ctx")
    packed = pack(pre_gate, values, quarters, spots, width)
    x = lax.all_to_all(packed.reshape(devices, width, BLK), both, 0, 0)
    mine = lax.axis_index("stretch")
    taps = lax.dynamic_slice_in_dim(filters, mine * groups, groups, 0)
    taps = jnp.pad(taps, ((0, 0), (BLK, BLK)))
    skip = lax.dynamic_slice_in_dim(skip_bias, mine * width, width, 0)
    tiles, near, skip = toeplitz(taps, skip)
    table = pair_table(doc_blocks, devices)
    mixed = conv(table, x, near, skip, tiles, group_width)
    back = lax.all_to_all(mixed, both, 0, 0)
    return finish(back.reshape(quarters, spots, width, BLK), post_gate)


def solution(mesh):
    in_specs = (
        P(("stretch", "ctx"), None),
        P(("stretch", "ctx"), None),
        P(("stretch", "ctx"), None),
        P("ctx", None),
        P("ctx"),
        P(),
    )
    return jax.shard_map(
        per_device, mesh=mesh, in_specs=in_specs, out_specs=P(("stretch", "ctx"), None), check_vma=False
    )
```

```python
import functools

import jax
import jax.numpy as jnp
from jax import lax
from jax.experimental import pallas as pl
from jax.experimental.pallas import tpu as pltpu
from jax.sharding import PartitionSpec as P

FLEN = 4096
BLK = 128
PAIR = 2 * BLK
LIGHT = 4
HEAVY = 9
UNITS = 8
VMEM_LIMIT = 16 << 20
BF = jnp.bfloat16
F32 = jnp.float32


def resident(x):
    return pltpu.with_memory_space_constraint(x, pltpu.VMEM)


def distant(x):
    return pltpu.with_memory_space_constraint(x, pltpu.HBM)


def pack_kernel(pre_ref, val_ref, out_ref, pre_buf, val_buf, out_buf, sems, *, pieces):
    quarters, spots, width, rows = out_ref.shape
    per = spots // pieces
    cols = per * quarters * width
    copies = []
    for k in range(pieces):
        part = pl.ds(k * cols, cols)
        pair = [
            pltpu.make_async_copy(src.at[:, part], dst.at[:, part], sems.at[k, i])
            for i, (src, dst) in enumerate(((pre_ref, pre_buf), (val_ref, val_buf)))
        ]
        for copy in pair:
            copy.start()
        copies.append(pair)
    for k in range(pieces):
        for copy in copies[k]:
            copy.wait()
        for i in range(k * per, (k + 1) * per):
            part = pl.ds(i * quarters * width, quarters * width)
            gated = (pre_buf[:, part].astype(F32) * val_buf[:, part].astype(F32)).astype(BF)
            out_buf[:, i] = gated.T.reshape(quarters, width, rows)
        part = pl.ds(k * per, per)
        copy = pltpu.make_async_copy(out_buf.at[:, part], out_ref.at[:, part], sems.at[k, 2])
        copy.start()
        copies[k] = [copy]
    for (copy,) in copies:
        copy.wait()


def pack(pre_gate, values, quarters, spots, width):
    rows, depth = values.shape
    pieces = 4
    whole = pl.BlockSpec(memory_space=pltpu.HBM)
    return pl.pallas_call(
        functools.partial(pack_kernel, pieces=pieces),
        in_specs=[whole, whole],
        out_specs=whole,
        out_shape=pltpu.HBM((quarters, spots, width, rows), BF),
        scratch_shapes=[
            pltpu.VMEM((rows, depth), BF),
            pltpu.VMEM((rows, depth), BF),
            pltpu.VMEM((quarters, spots, width, rows), BF),
            pltpu.SemaphoreType.DMA((pieces, 3)),
        ],
        compiler_params=pltpu.CompilerParams(vmem_limit_bytes=VMEM_LIMIT),
        name="pack",
    )(distant(pre_gate), distant(values))


def toeplitz_kernel(taps_ref, bias_ref, out_ref, near_ref, skip_ref):
    groups, tiles = out_ref.shape[:2]
    for g in range(groups):
        for k in range(tiles):
            if 1 <= k <= FLEN // BLK + 1:
                taps = taps_ref[g : g + 1, pl.ds((k - 1) * BLK, PAIR)]
                window = jnp.broadcast_to(taps, (BLK, PAIR))
                turned = pltpu.roll(window, 0, 1, stride=1, stride_axis=0)
                tile = turned[:, BLK:].astype(BF)
            else:
                tile = jnp.zeros((BLK, BLK), BF)
            out_ref[g, k] = tile
            if k < near_ref.shape[1]:
                near_ref[g, k] = tile
    skip_ref[...] = jnp.broadcast_to(bias_ref[...], (BLK, BLK)).T[: skip_ref.shape[0]]


def toeplitz(taps, bias):
    groups = taps.shape[0]
    width = bias.shape[0]
    return pl.pallas_call(
        toeplitz_kernel,
        out_shape=[
            jax.ShapeDtypeStruct((groups, FLEN // BLK + 3, BLK, BLK), BF),
            pltpu.VMEM((groups, 2 * LIGHT + 1, BLK, BLK), BF),
            pltpu.VMEM((width, BLK), F32),
        ],
        compiler_params=pltpu.CompilerParams(vmem_limit_bytes=VMEM_LIMIT),
        name="toeplitz",
    )(taps, jnp.pad(bias, (0, BLK - width))[None, :])


def conv_kernel(table_ref, x_ref, near_ref, skip_ref, tiles_hbm, out_ref, tiles_ref, acc_ref, sem, *, width, docs):
    groups = tiles_ref.shape[0]
    count, light = table_ref[3, 0], table_ref[4, 0]
    chunks = (count - docs + UNITS - 1) // UNITS
    spare = chunks * UNITS - (count - docs)
    last_lag = FLEN // PAIR
    last_blk = x_ref.shape[0] - 1
    load = pltpu.make_async_copy(tiles_hbm, tiles_ref, sem)
    load.start()

    def product(weights_ref, g, base, rank, start, lags):
        rows = pl.ds(g * width, width)
        zeros = jnp.zeros((width, BLK), BF)
        strips = []
        for u in range(len(base)):
            parts = []
            for i in range(lags):
                live = start + i <= rank[u]
                before = jnp.maximum(base[u] - 2 * (start + i), 0)
                after = jnp.minimum(before + 1, last_blk)
                for b in (before, after):
                    parts.append(jnp.where(live, x_ref[b, rows, :], zeros))
            strips.append(jnp.concatenate(parts, axis=1))
        left = jnp.concatenate(strips, axis=0)
        right = []
        for i in range(lags):
            k = 2 * (start + i) + 1
            right.append(jnp.concatenate([weights_ref[g, k], weights_ref[g, k + 1]], axis=1))
            right.append(jnp.concatenate([weights_ref[g, k - 1], weights_ref[g, k]], axis=1))
        right = jnp.concatenate(right, axis=0)
        return jnp.dot(left, right, preferred_element_type=F32)

    def store(g, total, base, second):
        rows = pl.ds(g * width, width)
        for u in range(len(base)):
            for half, b in ((1, second[u]), (0, base[u])):
                part = total[u * width : (u + 1) * width, half * BLK : (half + 1) * BLK]
                mixed = part + skip_ref[rows, :] * x_ref[b, rows, :].astype(F32)
                out_ref[b, rows, :] = mixed.astype(BF)

    def places(k):
        return [jnp.maximum(k * UNITS + u - spare, 0) + docs for u in range(UNITS)]

    def entries(k):
        return [[table_ref[row, p] for p in places(k)] for row in range(3)]

    def top(k):
        return table_ref[2, places(k)[-1]]

    def light_chunk(k, carry):
        lags = top(k) + 1
        for size in range(1, LIGHT + 1):

            @pl.when(lags == size)
            def _(size=size):
                base, second, rank = entries(k)
                for g in range(groups):
                    store(g, product(near_ref, g, base, rank, 0, size), base, second)

        return carry

    def heavy_chunk(k, carry):
        lags = jnp.minimum(top(k), last_lag) + 1
        whole = (lags - 1) // HEAVY

        def so_far(g, first):
            return jnp.where(first, 0.0, acc_ref[g])

        def lag_step(t, inner):
            base, _, rank = entries(k)
            for g in range(groups):
                acc_ref[g] = so_far(g, t == 0) + product(tiles_ref, g, base, rank, t * HEAVY, HEAVY)
            return inner

        lax.fori_loop(0, whole, lag_step, 0)
        for size in range(1, HEAVY + 1):

            @pl.when(lags - whole * HEAVY == size)
            def _(size=size):
                base, second, rank = entries(k)
                for g in range(groups):
                    total = so_far(g, whole == 0) + product(tiles_ref, g, base, rank, whole * HEAVY, size)
                    store(g, total, base, second)

        return carry

    firsts = [[table_ref[row, p] for p in range(docs)] for row in range(3)]
    for g in range(groups):
        store(g, product(near_ref, g, firsts[0], firsts[2], 0, 1), firsts[0], firsts[1])
    lax.fori_loop(0, light, light_chunk, 0)
    load.wait()
    lax.fori_loop(light, chunks, heavy_chunk, 0)


def conv(table, x, near, skip, tiles, width, docs):
    vmem = pl.BlockSpec(memory_space=pltpu.VMEM)
    hbm = pl.BlockSpec(memory_space=pltpu.HBM)
    return pl.pallas_call(
        functools.partial(conv_kernel, width=width, docs=docs),
        in_specs=[pl.BlockSpec(memory_space=pltpu.SMEM), vmem, vmem, vmem, hbm],
        out_specs=vmem,
        out_shape=pltpu.VMEM(x.shape, BF),
        scratch_shapes=[
            pltpu.VMEM(tiles.shape, BF),
            pltpu.VMEM((tiles.shape[0], UNITS * width, PAIR), F32),
            pltpu.SemaphoreType.DMA,
        ],
        compiler_params=pltpu.CompilerParams(vmem_limit_bytes=VMEM_LIMIT),
        name="conv",
    )(table, resident(x), resident(near), resident(skip), distant(tiles))


def finish_kernel(mixed_ref, post_ref, out_ref, buf, sems, *, pieces):
    quarters, spots, width, rows = mixed_ref.shape
    per = spots // pieces
    cols = per * quarters * width
    copies = []
    for k in range(pieces):
        for i in range(k * per, (k + 1) * per):
            part = pl.ds(i * quarters * width, quarters * width)
            mixed = mixed_ref[:, i].reshape(quarters * width, rows).T
            buf[:, part] = (post_ref[:, part].astype(F32) * mixed.astype(F32)).astype(BF)
        part = pl.ds(k * cols, cols)
        copy = pltpu.make_async_copy(buf.at[:, part], out_ref.at[:, part], sems.at[k])
        copy.start()
        copies.append(copy)
    for copy in copies:
        copy.wait()


def finish(mixed, post_gate):
    pieces = 8
    vmem = pl.BlockSpec(memory_space=pltpu.VMEM)
    return pl.pallas_call(
        functools.partial(finish_kernel, pieces=pieces),
        in_specs=[vmem, vmem],
        out_specs=pl.BlockSpec(memory_space=pltpu.HBM),
        out_shape=jax.ShapeDtypeStruct(post_gate.shape, BF),
        scratch_shapes=[pltpu.VMEM(post_gate.shape, BF), pltpu.SemaphoreType.DMA((pieces,))],
        compiler_params=pltpu.CompilerParams(vmem_limit_bytes=VMEM_LIMIT),
        name="finish",
    )(resident(mixed), resident(post_gate))


def pair_table(doc_blocks, all_blocks):
    docs = doc_blocks.shape[0]
    slots = (all_blocks + docs) // 2
    pairs = (doc_blocks + 1) // 2
    earlier = jnp.arange(docs)[:, None] < jnp.arange(docs)[None, :]
    doc_first = jnp.sum(jnp.where(earlier, doc_blocks[:, None], 0), axis=0)
    pair_first = jnp.sum(jnp.where(earlier, pairs[:, None], 0), axis=0)
    count = jnp.sum(pairs)
    slot = jnp.arange(slots, dtype=jnp.int32)
    mine = (slot[:, None] >= pair_first[None, :]) & (slot[:, None] < (pair_first + pairs)[None, :])
    place = slot[:, None] - pair_first[None, :]
    rank = jnp.sum(jnp.where(mine, place, 0), axis=1) + jnp.where(slot < count, 0, slots)
    base = jnp.sum(jnp.where(mine, doc_first[None, :] + 2 * place, 0), axis=1)
    both = jnp.sum(jnp.where(mine & (2 * place + 1 < doc_blocks[None, :]), 1, 0), axis=1)
    key = rank * slots + slot
    order = jnp.sum((key[None, :] < key[:, None]).astype(jnp.int32), axis=1)
    moved = order[None, :] == slot[:, None]
    columns = [jnp.sum(jnp.where(moved, c[None, :], 0), axis=1) for c in (base, base + both, rank)]
    light = (jnp.sum((rank < LIGHT).astype(jnp.int32)) - docs + (docs - count) % UNITS) // UNITS
    return jnp.stack(columns + [jnp.full((slots,), count), jnp.full((slots,), light)]).astype(jnp.int32)


def per_device(post_gate, pre_gate, values, filters, skip_bias, doc_blocks):
    quarters, spots = lax.axis_size("stretch"), lax.axis_size("ctx")
    devices = quarters * spots
    width = values.shape[1] // devices
    groups = filters.shape[0] // quarters
    group_width = width // groups
    both = ("stretch", "ctx")
    packed = pack(pre_gate, values, quarters, spots, width)
    x = lax.all_to_all(packed.reshape(devices, width, BLK), both, 0, 0)
    mine = lax.axis_index("stretch")
    taps = lax.dynamic_slice_in_dim(filters, mine * groups, groups, 0)
    taps = jnp.pad(taps, ((0, 0), (BLK, BLK)))
    skip = lax.dynamic_slice_in_dim(skip_bias, mine * width, width, 0)
    tiles, near, skip = toeplitz(taps, skip)
    table = pair_table(doc_blocks, devices)
    mixed = conv(table, x, near, skip, tiles, group_width, doc_blocks.shape[0])
    back = lax.all_to_all(mixed, both, 0, 0)
    return finish(back.reshape(quarters, spots, width, BLK), post_gate)


def solution(mesh):
    in_specs = (
        P(("stretch", "ctx"), None),
        P(("stretch", "ctx"), None),
        P(("stretch", "ctx"), None),
        P("ctx", None),
        P("ctx"),
        P(),
    )
    return jax.shard_map(
        per_device, mesh=mesh, in_specs=in_specs, out_specs=P(("stretch", "ctx"), None), check_vma=False
    )
```

```python
import functools

import jax
import jax.numpy as jnp
from jax import lax
from jax.experimental import pallas as pl
from jax.experimental.pallas import tpu as pltpu
from jax.sharding import PartitionSpec as P

FLEN = 4096
BLK = 128
PAIR = 2 * BLK
LIGHT = 4
HEAVY = 9
UNITS = 8
VMEM_LIMIT = 16 << 20
BF = jnp.bfloat16
F32 = jnp.float32


def resident(x):
    return pltpu.with_memory_space_constraint(x, pltpu.VMEM)


def distant(x):
    return pltpu.with_memory_space_constraint(x, pltpu.HBM)


def prepare_kernel(
    pre_ref, val_ref, taps_hbm, bias_hbm, docs_hbm, out_ref, tiles_ref, skip_ref, table_ref,
    pre_buf, val_buf, taps_ref, bias_ref, docs_ref, bias_buf, sems, small_sems, *, pieces,
):
    quarters, spots, width, rows = out_ref.shape
    groups, tiles = tiles_ref.shape[:2]
    per = spots // pieces
    cols = per * quarters * width
    small = [
        pltpu.make_async_copy(src, dst, small_sems.at[i])
        for i, (src, dst) in enumerate(((taps_hbm, taps_ref), (bias_hbm, bias_ref), (docs_hbm, docs_ref)))
    ]
    for copy in small:
        copy.start()
    copies = []
    for k in range(pieces):
        part = pl.ds(k * cols, cols)
        pair = [
            pltpu.make_async_copy(src.at[:, part], dst.at[:, part], sems.at[k, i])
            for i, (src, dst) in enumerate(((pre_ref, pre_buf), (val_ref, val_buf)))
        ]
        for copy in pair:
            copy.start()
        copies.append(pair)

    for copy in small:
        copy.wait()
    mine = lax.axis_index("stretch")
    held = taps_ref.shape[0]
    taps = pltpu.roll(taps_ref[...], lax.rem(held - mine * groups, held), 0)
    for g in range(groups):
        for k in range(tiles):
            j = k - 1
            if not 0 <= j <= FLEN // BLK:
                tiles_ref[g, k] = jnp.zeros((BLK, BLK), BF)
                continue
            halves = [
                taps[g : g + 1, i * BLK : (i + 1) * BLK] if 0 <= i < FLEN // BLK else jnp.zeros((1, BLK), F32)
                for i in (j - 1, j)
            ]
            window = jnp.broadcast_to(jnp.concatenate(halves, axis=1), (BLK, PAIR))
            turned = pltpu.roll(window, 0, 1, stride=1, stride_axis=0)
            tiles_ref[g, k] = turned[:, BLK:].astype(BF)

    across = BLK // width
    bias = jnp.zeros((1, BLK), F32)
    for i in range(bias_ref.shape[0]):
        bias = jnp.where(mine // across == i, bias_ref[i : i + 1, :], bias)
    bias = jnp.broadcast_to(bias, (BLK, BLK))
    bias_buf[...] = bias.T
    skip_ref[...] = bias_buf[pl.ds(pl.multiple_of(mine % across * width, width), width), :]

    docs = docs_ref.shape[0]
    blocks = [docs_ref[d] for d in range(docs)]
    pairs = [(n + 1) // 2 for n in blocks]
    most = (rows * spots * quarters // BLK + 1) // 2
    place = lax.broadcasted_iota(jnp.int32, (most, BLK), 0) + 1
    slot = lax.broadcasted_iota(jnp.int32, (most, BLK), 1)
    ahead = jnp.zeros((most, BLK), jnp.int32)
    for n in pairs:
        ahead = ahead + jnp.minimum(place, n)
    rank = jnp.sum((ahead <= slot).astype(jnp.int32), axis=0, keepdims=True)
    slot = lax.broadcasted_iota(jnp.int32, (1, BLK), 1)
    within = slot
    for n in pairs:
        within = within - jnp.minimum(rank, n)
    base = jnp.zeros((1, BLK), jnp.int32)
    second = jnp.zeros((1, BLK), jnp.int32)
    seen = jnp.zeros((1, BLK), jnp.int32)
    first = jnp.int32(0)
    for n, m in zip(blocks, pairs):
        holds = rank < m
        here = jnp.logical_and(holds, seen == within)
        start = first + 2 * rank
        base = jnp.where(here, start, base)
        second = jnp.where(here, jnp.minimum(start + 1, first + n - 1), second)
        seen = seen + holds.astype(jnp.int32)
        first = first + n
    count = functools.reduce(jnp.add, pairs)
    short = functools.reduce(jnp.add, [jnp.minimum(m, LIGHT) for m in pairs])
    rest = count - docs
    light = (short - docs + (rest + UNITS - 1) // UNITS * UNITS - rest) // UNITS
    lines = [base, second, rank, jnp.full((1, BLK), count, jnp.int32), jnp.full((1, BLK), light, jnp.int32)]
    for i, line in enumerate(lines):
        table_ref[i : i + 1, :] = line

    for k in range(pieces):
        for copy in copies[k]:
            copy.wait()
        for i in range(k * per, (k + 1) * per):
            part = pl.ds(i * quarters * width, quarters * width)
            gated = (pre_buf[:, part].astype(F32) * val_buf[:, part].astype(F32)).astype(BF)
            out_ref[:, i] = gated.T.reshape(quarters, width, rows)


def prepare(pre_gate, values, filters, skip_bias, doc_blocks, quarters, spots):
    rows, depth = values.shape
    width = depth // (quarters * spots)
    groups = filters.shape[0] // quarters
    pieces = 4
    bias = skip_bias.reshape(-1, BLK)
    hbm = pl.BlockSpec(memory_space=pltpu.HBM)
    vmem = pl.BlockSpec(memory_space=pltpu.VMEM)
    return pl.pallas_call(
        functools.partial(prepare_kernel, pieces=pieces),
        in_specs=[hbm] * 5,
        out_specs=[vmem] * 4,
        out_shape=[
            pltpu.VMEM((quarters, spots, width, rows), BF),
            pltpu.VMEM((groups, FLEN // BLK + 3, BLK, BLK), BF),
            pltpu.VMEM((width, BLK), F32),
            pltpu.VMEM((8, BLK), jnp.int32),
        ],
        scratch_shapes=[
            pltpu.VMEM((rows, depth), BF),
            pltpu.VMEM((rows, depth), BF),
            pltpu.VMEM(filters.shape, F32),
            pltpu.VMEM(bias.shape, F32),
            pltpu.SMEM(doc_blocks.shape, jnp.int32),
            pltpu.VMEM((BLK, BLK), F32),
            pltpu.SemaphoreType.DMA((pieces, 2)),
            pltpu.SemaphoreType.DMA((3,)),
        ],
        compiler_params=pltpu.CompilerParams(vmem_limit_bytes=VMEM_LIMIT),
        name="prepare",
    )(*[distant(a) for a in (pre_gate, values, filters, bias, doc_blocks)])


def conv_kernel(table_ref, x_ref, tiles_ref, skip_ref, out_ref, acc_ref, *, width, docs):
    groups = tiles_ref.shape[0]
    count, light = table_ref[3, 0], table_ref[4, 0]
    chunks = (count - docs + UNITS - 1) // UNITS
    spare = chunks * UNITS - (count - docs)
    last_lag = FLEN // PAIR
    last_blk = x_ref.shape[0] - 1

    def product(g, base, rank, start, lags):
        rows = pl.ds(g * width, width)
        zeros = jnp.zeros((width, BLK), BF)
        strips = []
        for u in range(len(base)):
            parts = []
            for i in range(lags):
                live = start + i <= rank[u]
                before = jnp.maximum(base[u] - 2 * (start + i), 0)
                after = jnp.minimum(before + 1, last_blk)
                for b in (before, after):
                    parts.append(jnp.where(live, x_ref[b, rows, :], zeros))
            strips.append(jnp.concatenate(parts, axis=1))
        left = jnp.concatenate(strips, axis=0)
        right = []
        for i in range(lags):
            k = 2 * (start + i) + 1
            right.append(jnp.concatenate([tiles_ref[g, k], tiles_ref[g, k + 1]], axis=1))
            right.append(jnp.concatenate([tiles_ref[g, k - 1], tiles_ref[g, k]], axis=1))
        right = jnp.concatenate(right, axis=0)
        return jnp.dot(left, right, preferred_element_type=F32)

    def store(g, total, base, second):
        rows = pl.ds(g * width, width)
        for u in range(len(base)):
            for half, b in ((1, second[u]), (0, base[u])):
                part = total[u * width : (u + 1) * width, half * BLK : (half + 1) * BLK]
                mixed = part + skip_ref[rows, :] * x_ref[b, rows, :].astype(F32)
                out_ref[b, rows, :] = mixed.astype(BF)

    def places(k):
        return [jnp.maximum(k * UNITS + u - spare, 0) + docs for u in range(UNITS)]

    def entries(k):
        return [[table_ref[row, p] for p in places(k)] for row in range(3)]

    def top(k):
        return table_ref[2, places(k)[-1]]

    def light_chunk(k, carry):
        lags = top(k) + 1
        for size in range(1, LIGHT + 1):

            @pl.when(lags == size)
            def _(size=size):
                base, second, rank = entries(k)
                for g in range(groups):
                    store(g, product(g, base, rank, 0, size), base, second)

        return carry

    def heavy_chunk(k, carry):
        lags = jnp.minimum(top(k), last_lag) + 1
        whole = (lags - 1) // HEAVY

        def so_far(g, first):
            return jnp.where(first, 0.0, acc_ref[g])

        def lag_step(t, inner):
            base, _, rank = entries(k)
            for g in range(groups):
                acc_ref[g] = so_far(g, t == 0) + product(g, base, rank, t * HEAVY, HEAVY)
            return inner

        lax.fori_loop(0, whole, lag_step, 0)
        for size in range(1, HEAVY + 1):

            @pl.when(lags - whole * HEAVY == size)
            def _(size=size):
                base, second, rank = entries(k)
                for g in range(groups):
                    total = so_far(g, whole == 0) + product(g, base, rank, whole * HEAVY, size)
                    store(g, total, base, second)

        return carry

    firsts = [[table_ref[row, p] for p in range(docs)] for row in range(3)]
    for g in range(groups):
        store(g, product(g, firsts[0], firsts[2], 0, 1), firsts[0], firsts[1])
    lax.fori_loop(0, light, light_chunk, 0)
    lax.fori_loop(light, chunks, heavy_chunk, 0)


def conv(table, x, tiles, skip, width, docs):
    vmem = pl.BlockSpec(memory_space=pltpu.VMEM)
    return pl.pallas_call(
        functools.partial(conv_kernel, width=width, docs=docs),
        in_specs=[pl.BlockSpec(memory_space=pltpu.SMEM), vmem, vmem, vmem],
        out_specs=vmem,
        out_shape=pltpu.VMEM(x.shape, BF),
        scratch_shapes=[pltpu.VMEM((tiles.shape[0], UNITS * width, PAIR), F32)],
        compiler_params=pltpu.CompilerParams(vmem_limit_bytes=VMEM_LIMIT),
        name="conv",
    )(table, resident(x), resident(tiles), resident(skip))


def finish_kernel(mixed_ref, post_ref, out_ref, buf, sems, *, pieces):
    quarters, spots, width, rows = mixed_ref.shape
    per = spots // pieces
    cols = per * quarters * width
    copies = []
    for k in range(pieces):
        for i in range(k * per, (k + 1) * per):
            part = pl.ds(i * quarters * width, quarters * width)
            mixed = mixed_ref[:, i].reshape(quarters * width, rows).T
            buf[:, part] = (post_ref[:, part].astype(F32) * mixed.astype(F32)).astype(BF)
        part = pl.ds(k * cols, cols)
        copy = pltpu.make_async_copy(buf.at[:, part], out_ref.at[:, part], sems.at[k])
        copy.start()
        copies.append(copy)
    for copy in copies:
        copy.wait()


def finish(mixed, post_gate):
    pieces = 8
    vmem = pl.BlockSpec(memory_space=pltpu.VMEM)
    return pl.pallas_call(
        functools.partial(finish_kernel, pieces=pieces),
        in_specs=[vmem, vmem],
        out_specs=pl.BlockSpec(memory_space=pltpu.HBM),
        out_shape=jax.ShapeDtypeStruct(post_gate.shape, BF),
        scratch_shapes=[pltpu.VMEM(post_gate.shape, BF), pltpu.SemaphoreType.DMA((pieces,))],
        compiler_params=pltpu.CompilerParams(vmem_limit_bytes=VMEM_LIMIT),
        name="finish",
    )(resident(mixed), resident(post_gate))


def per_device(post_gate, pre_gate, values, filters, skip_bias, doc_blocks):
    quarters, spots = lax.axis_size("stretch"), lax.axis_size("ctx")
    both = ("stretch", "ctx")
    packed, tiles, skip, table = prepare(pre_gate, values, filters, skip_bias, doc_blocks, quarters, spots)
    width = packed.shape[2]
    x = lax.all_to_all(packed.reshape(quarters * spots, width, BLK), both, 0, 0)
    mixed = conv(table, x, tiles, skip, width // tiles.shape[0], doc_blocks.shape[0])
    back = lax.all_to_all(mixed, both, 0, 0)
    return finish(back.reshape(quarters, spots, width, BLK), post_gate)


def solution(mesh):
    in_specs = (
        P(("stretch", "ctx"), None),
        P(("stretch", "ctx"), None),
        P(("stretch", "ctx"), None),
        P("ctx", None),
        P("ctx"),
        P(),
    )
    return jax.shard_map(
        per_device, mesh=mesh, in_specs=in_specs, out_specs=P(("stretch", "ctx"), None), check_vma=False
    )
```

```python
import functools

import jax
import jax.numpy as jnp
from jax import lax
from jax.experimental import pallas as pl
from jax.experimental.pallas import tpu as pltpu
from jax.sharding import PartitionSpec as P

FLEN = 4096
BLK = 128
PAIR = 2 * BLK
LIGHT = 4
HEAVY = 9
UNITS = 8
VMEM_LIMIT = 16 << 20
BF = jnp.bfloat16
F32 = jnp.float32


def resident(x):
    return pltpu.with_memory_space_constraint(x, pltpu.VMEM)


def distant(x):
    return pltpu.with_memory_space_constraint(x, pltpu.HBM)


def prepare_kernel(
    pre_ref, val_ref, taps_hbm, bias_hbm, docs_hbm, out_ref, tiles_ref, skip_ref, table_ref,
    pre_buf, val_buf, taps_ref, bias_ref, docs_ref, bias_buf, sems, small_sems, *, pieces,
):
    quarters, spots, width, rows = out_ref.shape
    groups, tiles = tiles_ref.shape[:2]
    per = spots // pieces
    cols = per * quarters * width
    small = [
        pltpu.make_async_copy(src, dst, small_sems.at[i])
        for i, (src, dst) in enumerate(((taps_hbm, taps_ref), (bias_hbm, bias_ref), (docs_hbm, docs_ref)))
    ]
    for copy in small:
        copy.start()
    copies = []
    for k in range(pieces):
        part = pl.ds(k * cols, cols)
        pair = [
            pltpu.make_async_copy(src.at[:, part], dst.at[:, part], sems.at[k, i])
            for i, (src, dst) in enumerate(((pre_ref, pre_buf), (val_ref, val_buf)))
        ]
        for copy in pair:
            copy.start()
        copies.append(pair)

    for copy in small:
        copy.wait()
    mine = lax.axis_index("stretch")
    held = taps_ref.shape[0]
    taps = pltpu.roll(taps_ref[...], lax.rem(held - mine * groups, held), 0)
    lower = lax.broadcasted_iota(jnp.int32, (BLK, BLK), 0) <= lax.broadcasted_iota(jnp.int32, (BLK, BLK), 1)
    last = FLEN // BLK
    for g in range(groups):
        tiles_ref[g, 0] = jnp.zeros((BLK, BLK), BF)
        tiles_ref[g, tiles - 1] = jnp.zeros((BLK, BLK), BF)
        before = None
        for j in range(0, last + 1, 2):
            halves = [
                taps[g : g + 1, i * BLK : (i + 1) * BLK] if 0 <= i < last else jnp.zeros((1, BLK), F32)
                for i in (j - 1, j)
            ]
            window = jnp.broadcast_to(jnp.concatenate(halves, axis=1), (BLK, PAIR))
            turned = pltpu.roll(window, 0, 1, stride=1, stride_axis=0)
            tiles_ref[g, j + 1] = turned[:, BLK:].astype(BF)
            if before is not None:
                tiles_ref[g, j] = jnp.where(lower, turned[:, :BLK], before).astype(BF)
            before = turned[:, :BLK]

    across = BLK // width
    bias = jnp.zeros((1, BLK), F32)
    for i in range(bias_ref.shape[0]):
        bias = jnp.where(mine // across == i, bias_ref[i : i + 1, :], bias)
    bias = jnp.broadcast_to(bias, (BLK, BLK))
    bias_buf[...] = bias.T
    skip_ref[...] = bias_buf[pl.ds(pl.multiple_of(mine % across * width, width), width), :]

    docs = docs_ref.shape[0]
    blocks = [docs_ref[d] for d in range(docs)]
    pairs = [(n + 1) // 2 for n in blocks]
    most = (rows * spots * quarters // BLK + 1) // 2
    place = lax.broadcasted_iota(jnp.int32, (most, BLK), 0) + 1
    slot = lax.broadcasted_iota(jnp.int32, (most, BLK), 1)
    ahead = jnp.zeros((most, BLK), jnp.int32)
    for n in pairs:
        ahead = ahead + jnp.minimum(place, n)
    rank = jnp.sum((ahead <= slot).astype(jnp.int32), axis=0, keepdims=True)
    slot = lax.broadcasted_iota(jnp.int32, (1, BLK), 1)
    within = slot
    for n in pairs:
        within = within - jnp.minimum(rank, n)
    base = jnp.zeros((1, BLK), jnp.int32)
    second = jnp.zeros((1, BLK), jnp.int32)
    seen = jnp.zeros((1, BLK), jnp.int32)
    first = jnp.int32(0)
    for n, m in zip(blocks, pairs):
        holds = rank < m
        here = jnp.logical_and(holds, seen == within)
        start = first + 2 * rank
        base = jnp.where(here, start, base)
        second = jnp.where(here, jnp.minimum(start + 1, first + n - 1), second)
        seen = seen + holds.astype(jnp.int32)
        first = first + n
    count = functools.reduce(jnp.add, pairs)
    short = functools.reduce(jnp.add, [jnp.minimum(m, LIGHT) for m in pairs])
    rest = count - docs
    light = (short - docs + (rest + UNITS - 1) // UNITS * UNITS - rest) // UNITS
    lines = [base, second, rank, jnp.full((1, BLK), count, jnp.int32), jnp.full((1, BLK), light, jnp.int32)]
    for i, line in enumerate(lines):
        table_ref[i : i + 1, :] = line

    for k in range(pieces):
        for copy in copies[k]:
            copy.wait()
        for i in range(k * per, (k + 1) * per):
            part = pl.ds(i * quarters * width, quarters * width)
            gated = (pre_buf[:, part].astype(F32) * val_buf[:, part].astype(F32)).astype(BF)
            out_ref[:, i] = gated.T.reshape(quarters, width, rows)


def prepare(pre_gate, values, filters, skip_bias, doc_blocks, quarters, spots):
    rows, depth = values.shape
    width = depth // (quarters * spots)
    groups = filters.shape[0] // quarters
    pieces = 4
    bias = skip_bias.reshape(-1, BLK)
    hbm = pl.BlockSpec(memory_space=pltpu.HBM)
    vmem = pl.BlockSpec(memory_space=pltpu.VMEM)
    return pl.pallas_call(
        functools.partial(prepare_kernel, pieces=pieces),
        in_specs=[hbm] * 5,
        out_specs=[vmem] * 4,
        out_shape=[
            pltpu.VMEM((quarters, spots, width, rows), BF),
            pltpu.VMEM((groups, FLEN // BLK + 3, BLK, BLK), BF),
            pltpu.VMEM((width, BLK), F32),
            pltpu.VMEM((8, BLK), jnp.int32),
        ],
        scratch_shapes=[
            pltpu.VMEM((rows, depth), BF),
            pltpu.VMEM((rows, depth), BF),
            pltpu.VMEM(filters.shape, F32),
            pltpu.VMEM(bias.shape, F32),
            pltpu.SMEM(doc_blocks.shape, jnp.int32),
            pltpu.VMEM((BLK, BLK), F32),
            pltpu.SemaphoreType.DMA((pieces, 2)),
            pltpu.SemaphoreType.DMA((3,)),
        ],
        compiler_params=pltpu.CompilerParams(vmem_limit_bytes=VMEM_LIMIT),
        name="prepare",
    )(*[distant(a) for a in (pre_gate, values, filters, bias, doc_blocks)])


def conv_kernel(table_ref, x_ref, tiles_ref, skip_ref, out_ref, acc_ref, *, width, docs):
    groups = tiles_ref.shape[0]
    count, light = table_ref[3, 0], table_ref[4, 0]
    chunks = (count - docs + UNITS - 1) // UNITS
    spare = chunks * UNITS - (count - docs)
    last_lag = FLEN // PAIR
    last_blk = x_ref.shape[0] - 1

    def product(g, base, rank, start, lags):
        rows = pl.ds(g * width, width)
        zeros = jnp.zeros((width, BLK), BF)
        strips = []
        for u in range(len(base)):
            parts = []
            for i in range(lags):
                live = start + i <= rank[u]
                before = jnp.maximum(base[u] - 2 * (start + i), 0)
                after = jnp.minimum(before + 1, last_blk)
                for b in (before, after):
                    parts.append(jnp.where(live, x_ref[b, rows, :], zeros))
            strips.append(jnp.concatenate(parts, axis=1))
        left = jnp.concatenate(strips, axis=0)
        right = []
        for i in range(lags):
            k = 2 * (start + i) + 1
            right.append(jnp.concatenate([tiles_ref[g, k], tiles_ref[g, k + 1]], axis=1))
            right.append(jnp.concatenate([tiles_ref[g, k - 1], tiles_ref[g, k]], axis=1))
        right = jnp.concatenate(right, axis=0)
        return jnp.dot(left, right, preferred_element_type=F32)

    def store(g, total, base, second):
        rows = pl.ds(g * width, width)
        for u in range(len(base)):
            for half, b in ((1, second[u]), (0, base[u])):
                part = total[u * width : (u + 1) * width, half * BLK : (half + 1) * BLK]
                mixed = part + skip_ref[rows, :] * x_ref[b, rows, :].astype(F32)
                out_ref[b, rows, :] = mixed.astype(BF)

    def places(k):
        return [jnp.maximum(k * UNITS + u - spare, 0) + docs for u in range(UNITS)]

    def entries(k):
        return [[table_ref[row, p] for p in places(k)] for row in range(3)]

    def top(k):
        return table_ref[2, places(k)[-1]]

    def light_chunk(k, carry):
        lags = top(k) + 1
        for size in range(1, LIGHT + 1):

            @pl.when(lags == size)
            def _(size=size):
                base, second, rank = entries(k)
                for g in range(groups):
                    store(g, product(g, base, rank, 0, size), base, second)

        return carry

    def heavy_chunk(k, carry):
        lags = jnp.minimum(top(k), last_lag) + 1
        whole = (lags - 1) // HEAVY

        def so_far(g, first):
            return jnp.where(first, 0.0, acc_ref[g])

        def lag_step(t, inner):
            base, _, rank = entries(k)
            for g in range(groups):
                acc_ref[g] = so_far(g, t == 0) + product(g, base, rank, t * HEAVY, HEAVY)
            return inner

        lax.fori_loop(0, whole, lag_step, 0)
        for size in range(1, HEAVY + 1):

            @pl.when(lags - whole * HEAVY == size)
            def _(size=size):
                base, second, rank = entries(k)
                for g in range(groups):
                    total = so_far(g, whole == 0) + product(g, base, rank, whole * HEAVY, size)
                    store(g, total, base, second)

        return carry

    firsts = [[table_ref[row, p] for p in range(docs)] for row in range(3)]
    for g in range(groups):
        store(g, product(g, firsts[0], firsts[2], 0, 1), firsts[0], firsts[1])
    lax.fori_loop(0, light, light_chunk, 0)
    lax.fori_loop(light, chunks, heavy_chunk, 0)


def conv(table, x, tiles, skip, width, docs):
    vmem = pl.BlockSpec(memory_space=pltpu.VMEM)
    return pl.pallas_call(
        functools.partial(conv_kernel, width=width, docs=docs),
        in_specs=[pl.BlockSpec(memory_space=pltpu.SMEM), vmem, vmem, vmem],
        out_specs=vmem,
        out_shape=pltpu.VMEM(x.shape, BF),
        scratch_shapes=[pltpu.VMEM((tiles.shape[0], UNITS * width, PAIR), F32)],
        compiler_params=pltpu.CompilerParams(vmem_limit_bytes=VMEM_LIMIT),
        name="conv",
    )(table, resident(x), resident(tiles), resident(skip))


def finish_kernel(mixed_ref, post_ref, out_ref, buf, sems, *, pieces):
    quarters, spots, width, rows = mixed_ref.shape
    per = spots // pieces
    cols = per * quarters * width
    copies = []
    for k in range(pieces):
        for i in range(k * per, (k + 1) * per):
            part = pl.ds(i * quarters * width, quarters * width)
            mixed = mixed_ref[:, i].reshape(quarters * width, rows).T
            buf[:, part] = (post_ref[:, part].astype(F32) * mixed.astype(F32)).astype(BF)
        part = pl.ds(k * cols, cols)
        copy = pltpu.make_async_copy(buf.at[:, part], out_ref.at[:, part], sems.at[k])
        copy.start()
        copies.append(copy)
    for copy in copies:
        copy.wait()


def finish(mixed, post_gate):
    pieces = 8
    vmem = pl.BlockSpec(memory_space=pltpu.VMEM)
    return pl.pallas_call(
        functools.partial(finish_kernel, pieces=pieces),
        in_specs=[vmem, vmem],
        out_specs=pl.BlockSpec(memory_space=pltpu.HBM),
        out_shape=jax.ShapeDtypeStruct(post_gate.shape, BF),
        scratch_shapes=[pltpu.VMEM(post_gate.shape, BF), pltpu.SemaphoreType.DMA((pieces,))],
        compiler_params=pltpu.CompilerParams(vmem_limit_bytes=VMEM_LIMIT),
        name="finish",
    )(resident(mixed), resident(post_gate))


def per_device(post_gate, pre_gate, values, filters, skip_bias, doc_blocks):
    quarters, spots = lax.axis_size("stretch"), lax.axis_size("ctx")
    both = ("stretch", "ctx")
    packed, tiles, skip, table = prepare(pre_gate, values, filters, skip_bias, doc_blocks, quarters, spots)
    width = packed.shape[2]
    x = lax.all_to_all(packed.reshape(quarters * spots, width, BLK), both, 0, 0)
    mixed = conv(table, x, tiles, skip, width // tiles.shape[0], doc_blocks.shape[0])
    back = lax.all_to_all(mixed, both, 0, 0)
    return finish(back.reshape(quarters, spots, width, BLK), post_gate)


def solution(mesh):
    in_specs = (
        P(("stretch", "ctx"), None),
        P(("stretch", "ctx"), None),
        P(("stretch", "ctx"), None),
        P("ctx", None),
        P("ctx"),
        P(),
    )
    return jax.shard_map(
        per_device, mesh=mesh, in_specs=in_specs, out_specs=P(("stretch", "ctx"), None), check_vma=False
    )
```
